256 devices in a mesh: dp: 16 (over x_lo, z), shard: 16 (over x_hi, y, core).
Axes of the slice: x: 4 (x_hi: 2, x_lo: 2; x = x_hi * 2 + x_lo), y: 4, z: 8, core: 2. Of those that a mesh axis runs over, the one named last changes fastest.
Arguments:
- gradient: bfloat16 [16, 2560, 2560], P(None, ('shard', 'dp')), may hold values from -1.5 to 1.5
- owner: int32 [16], replicated, may hold values from 0 to 15, each once
- a_inverse: bfloat16 [16, 2560, 2560], P('dp', 'shard'), as said below
- b_inverse: bfloat16 [16, 2560, 2560], P('dp', 'shard'), as said below
Outputs:
- preconditioned: bfloat16 [16, 2560, 2560], P(None, ('shard', 'dp'))
The draws below stay inside these ranges and needn't reach their ends.
Inputs may be any that keep to these rules, and one draw needn't show every extreme that they name: owner names each of the 16 slots for exactly one layer. Every slot of a_inverse is a symmetric matrix. Every slot of b_inverse is a symmetric matrix.
All inputs are finite; a program needn't handle non-finite values.
Results may differ from the reference program's by a relative error of at most 0.0049.
Values may be sent and summed in bfloat16 or wider, within the bound.
No kernel may reach another device: no remote copies, remote signals or barrier semaphores. Data moves between devices by JAX's collectives and lax.ppermute only.
A program may use at most 128 MiB of HBM per device.

```python
import math
import jax
import jax.numpy as jnp
from jax import lax

DIM = 2560
LAYERS = 16


def factor_draw(key):
    first_key, second_key = jax.random.split(key, 2)
    noise = jax.random.normal(first_key, (LAYERS, DIM, DIM), jnp.float32)
    diagonal = jnp.exp(jax.random.uniform(second_key, (LAYERS, DIM), jnp.float32, math.log(1.5), math.log(4.0)))
    symmetric = (noise + jnp.swapaxes(noise, 1, 2)) * (0.6 / math.sqrt(2.0 * DIM))
    identity = jnp.eye(DIM, dtype=jnp.float32)
    return (symmetric + identity[None, :, :] * diagonal[:, None, :]).astype(jnp.bfloat16)


def draw_a_inverse(key, part):
    return factor_draw(jax.random.fold_in(key, 11))


def draw_b_inverse(key, part):
    return factor_draw(jax.random.fold_in(key, 23))


def steps_of(rng, extent, cuts, low, largest):
    factor_of = 1.0
    for dim, parts in cuts:
        heights = jax.random.uniform(jax.random.fold_in(jax.random.fold_in(rng, 6), dim), (parts,), jnp.float32, low / len(cuts), largest / len(cuts))
        factor_of = factor_of * jnp.repeat(jnp.exp(heights), extent[dim] // parts).reshape((-1,) + (1,) * (len(extent) - 1 - dim))
    return factor_of


def scatter_about(own_key, extent, deviation, bound, pieces=(), kind=jnp.bfloat16):
    drawn = deviation * jax.random.normal(own_key, extent, jnp.float32)
    if pieces:
        drawn = drawn * steps_of(own_key, extent, pieces, -0.22, 0.18)
    return jnp.clip(drawn, -bound, bound).astype(kind)


def setup_inputs(seed: int = 0) -> dict:
    key_list = jax.random.split(jax.random.key(seed), 5)
    return {
        "gradient": scatter_about(key_list[0], (LAYERS, DIM, DIM), 0.25, 1.5, ((1, 256),)),
        "owner": jax.random.permutation(key_list[1], LAYERS).astype(jnp.int32),
        "a_inverse": draw_a_inverse(jax.random.fold_in(key_list[4], 71), 0),
        "b_inverse": draw_b_inverse(jax.random.fold_in(key_list[4], 71), 0),
    }


def reference(gradient, owner, a_inverse, b_inverse):
    def one_layer(layer_index):
        holder = owner[layer_index]
        right_half = jnp.dot(gradient[layer_index], b_inverse[holder], preferred_element_type=jnp.float32).astype(jnp.bfloat16)
        return jnp.dot(a_inverse[holder], right_half, preferred_element_type=jnp.float32).astype(jnp.bfloat16)

    return lax.map(one_layer, jnp.arange(LAYERS, dtype=jnp.int32))
```

```python
import jax
import jax.numpy as jnp
from jax import lax
from jax.experimental import pallas as pl
from jax.experimental.pallas import tpu as pltpu
from jax.sharding import Mesh, PartitionSpec as P

AXES = ("xl", "z", "xh", "y", "c")
SIZES = dict(xl=2, z=8, xh=2, y=4, c=2)
DP = ("xl", "z")
ROWS = 10
SLOTS = 16
BLOCK = ROWS * SLOTS
PARTS = 4
VMEM_LIMIT = 48 * 1024 * 1024
F32 = jnp.float32
BF16 = jnp.bfloat16


def shift(value, axis, by):
    n = SIZES[axis]
    return lax.ppermute(value, axis, [(i, (i + by) % n) for i in range(n)])


def params():
    return pltpu.CompilerParams(vmem_limit_bytes=VMEM_LIMIT)


def onehot(hit):
    return jnp.where(hit, 1.0, 0.0).astype(BF16)


def vspec():
    return pl.BlockSpec(memory_space=pltpu.VMEM)


def aspec():
    return pl.BlockSpec(memory_space=pl.ANY)


def sspec():
    return pl.BlockSpec(memory_space=pltpu.SMEM)


def pack_kernel(base_ref, part_ref, *refs):
    x_refs, o_ref = refs[:-1], refs[-1]
    rows = PARTS * BLOCK
    width = o_ref.shape[1]
    row = lax.broadcasted_iota(jnp.int32, (rows, BLOCK), 0)
    total = None
    for q in range(PARTS):
        pick = onehot(row == base_ref[...] + ROWS * part_ref[q])
        x = x_refs[q][...] if len(x_refs) > 1 else x_refs[0][:, q * width : (q + 1) * width]
        term = jnp.dot(pick, x, preferred_element_type=F32)
        total = term if total is None else total + term
    o_ref[...] = total.astype(BF16)


def pack(base, parts, xs):
    width = 640
    return pl.pallas_call(
        pack_kernel,
        out_shape=jax.ShapeDtypeStruct((PARTS * BLOCK, width), BF16),
        in_specs=[vspec(), sspec()] + [vspec()] * len(xs),
        out_specs=vspec(),
        compiler_params=params(),
        name="pack",
    )(base, parts, *xs)


def unpack_kernel(interleave, base_ref, x_ref, o_ref):
    width = x_ref.shape[1]
    col = lax.broadcasted_iota(jnp.int32, (BLOCK, PARTS * BLOCK), 1)
    for q in range(PARTS):
        pick = onehot(col == base_ref[...] + ROWS * q)
        block = jnp.dot(pick, x_ref[...], preferred_element_type=F32)
        if not interleave:
            o_ref[:, q * width : (q + 1) * width] = block.astype(BF16)
            continue
        xh, c = q // 2, q % 2
        for y in range(4):
            at = (xh * 8 + y * 2 + c) * BLOCK
            o_ref[:, at : at + BLOCK] = block[:, y * BLOCK : (y + 1) * BLOCK].astype(BF16)


def unpack(base, x, interleave):
    import functools

    return pl.pallas_call(
        functools.partial(unpack_kernel, interleave),
        out_shape=jax.ShapeDtypeStruct((BLOCK, PARTS * x.shape[1]), BF16),
        in_specs=[vspec(), vspec()],
        out_specs=vspec(),
        compiler_params=params(),
        name="unpack",
    )(base, x)


def right_kernel(count, at_ref, *refs):
    g_refs, b_refs = refs[:count], refs[count : count + 4]
    o_refs, (b_all, sem) = refs[count + 4 : 2 * count + 4], refs[2 * count + 4 :]
    copies = [
        pltpu.make_async_copy(b, b_all.at[pl.ds(pl.multiple_of(at_ref[n], 32), BLOCK)], sem.at[n])
        for n, b in enumerate(b_refs)
    ]
    for copy in copies:
        copy.start()
    for copy in copies:
        copy.wait()
    for g, o in zip(g_refs, o_refs):
        o[...] = lax.dot_general(
            g[...], b_all[...], (((1,), (1,)), ((), ())), preferred_element_type=F32
        ).astype(BF16)


def right(at, gs, bs):
    import functools

    n = len(gs)
    return pl.pallas_call(
        functools.partial(right_kernel, n),
        out_shape=[jax.ShapeDtypeStruct((BLOCK, 4 * BLOCK), BF16)] * n,
        in_specs=[sspec()] + [vspec()] * n + [aspec()] * 4,
        out_specs=[vspec()] * n,
        scratch_shapes=[pltpu.VMEM((4 * BLOCK, gs[0].shape[1]), BF16), pltpu.SemaphoreType.DMA((4,))],
        compiler_params=params(),
        cost_estimate=pl.CostEstimate(
            flops=2 * n * BLOCK * 640 * 2560, bytes_accessed=(n + 4) * BLOCK * 2560 * 2, transcendentals=0
        ),
        name="right",
    )(at, *gs, *bs)


def left_kernel(count, at_ref, *refs):
    a_refs, r_refs = refs[:count], refs[count : count + 16]
    o_refs, (r_all, sem) = refs[count + 16 : 2 * count + 16], refs[2 * count + 16 :]
    copies = [
        pltpu.make_async_copy(r, r_all.at[pl.ds(pl.multiple_of(at_ref[n], 32), BLOCK)], sem.at[n])
        for n, r in enumerate(r_refs)
    ]
    for copy in copies:
        copy.start()
    for copy in copies:
        copy.wait()
    for a, o in zip(a_refs, o_refs):
        o[...] = jnp.dot(a[...], r_all[...], preferred_element_type=F32).astype(BF16)


def left(at, blocks, rs):
    import functools

    n = len(blocks)
    return pl.pallas_call(
        functools.partial(left_kernel, n),
        out_shape=[jax.ShapeDtypeStruct((BLOCK, 4 * BLOCK), BF16)] * n,
        in_specs=[sspec()] + [vspec()] * n + [aspec()] * 16,
        out_specs=[vspec()] * n,
        scratch_shapes=[pltpu.VMEM((16 * BLOCK, 4 * BLOCK), BF16), pltpu.SemaphoreType.DMA((16,))],
        compiler_params=params(),
        cost_estimate=pl.CostEstimate(
            flops=2 * n * BLOCK * 640 * 2560, bytes_accessed=(n + 4) * BLOCK * 2560 * 2, transcendentals=0
        ),
        name="left",
    )(at, *blocks, *rs)


def around(value):
    over_x = shift(value, "xh", 1)
    return [value, shift(value, "c", 1), over_x, shift(over_x, "c", 1)]


def along(value):
    return [value, shift(value, "y", 1), shift(value, "y", -1), shift(value, "y", 2)]


def exchange(x):
    width = x.shape[1]
    x = x.reshape(SLOTS, PARTS * ROWS, width)
    return lax.all_to_all(x, DP, split_axis=0, concat_axis=0, tiled=True).reshape(-1, width)


def local(gradient, owner, a_inverse, b_inverse):
    xh, y, c = (lax.axis_index(n) for n in ("xh", "y", "c"))
    a, b = a_inverse[0], b_inverse[0]
    features = gradient.shape[2]
    m = jnp.arange(BLOCK, dtype=jnp.int32)
    natural = (m // ROWS) * (PARTS * ROWS) + m % ROWS
    by_layer = jnp.tile(owner, ROWS) * (PARTS * ROWS) + m // SLOTS
    in_order = jnp.arange(PARTS, dtype=jnp.int32)
    near = [(xh, c), (xh, 1 - c), (1 - xh, c), (1 - xh, 1 - c)]
    ys = [y, (y + 3) % 4, (y + 1) % 4, (y + 2) % 4]

    rows = gradient.transpose(1, 0, 2).reshape(BLOCK, features)
    bs = along(b)
    g = unpack(natural[:, None], exchange(pack(by_layer[None, :], in_order, [rows])), False)
    blocks = around(a)
    r = right(jnp.stack(ys).astype(jnp.int32) * BLOCK, around(g), bs)
    moved = [along(v) for v in r]
    at = jnp.stack([(u * 8 + v * 2 + w) * BLOCK for u, w in near for v in ys]).astype(jnp.int32)
    out = left(at, blocks, [moved[n][k] for n in range(4) for k in range(4)])
    swap = lambda v: lax.ppermute(v, ("xh", "c"), [(i, 3 - i) for i in range(4)])
    mine = [out[0], shift(out[1], "c", 1), shift(out[2], "xh", 1), swap(out[3])]
    parts = jnp.stack([u * 2 + w for u, w in near]).astype(jnp.int32)
    done = unpack(by_layer[:, None], exchange(pack(natural[None, :], parts, mine)), True)
    return done.reshape(ROWS, SLOTS, features).transpose(1, 0, 2)


def solution(mesh):
    fine = Mesh(mesh.devices.reshape(tuple(SIZES[n] for n in AXES)), AXES)
    rows = ("xh", "y", "c")
    in_specs = (P(None, rows + DP, None), P(), P(DP, rows, None), P(DP, rows, None))
    return jax.shard_map(
        local, mesh=fine, in_specs=in_specs, out_specs=P(None, rows + DP, None), check_vma=False
    )
```

```python
import functools

import jax
import jax.numpy as jnp
from jax import lax
from jax.experimental import pallas as pl
from jax.experimental.pallas import tpu as pltpu
from jax.sharding import Mesh, PartitionSpec as P

AXES = ("xl", "z", "xh", "y", "c")
SIZES = dict(xl=2, z=8, xh=2, y=4, c=2)
DP = ("xl", "z")
NEAR = ("xh", "c")
LAYERS = 16
ROWS = 10
BLOCK = ROWS * LAYERS
PARTS = 4
WIDE = 2560
COLS = WIDE // PARTS
F32 = jnp.float32
BF16 = jnp.bfloat16

TO, PART, BAT, RAT, SIDE = 0, 16, 20, 25, 41


def shift(value, axis, by):
    n = SIZES[axis]
    return lax.ppermute(value, axis, [(i, (i + by) % n) for i in range(n)])


def flip(value, mask):
    return lax.ppermute(value, NEAR, [(i, i ^ mask) for i in range(4)])


def params(mib):
    return pltpu.CompilerParams(vmem_limit_bytes=mib * 1024 * 1024)


def cost(flops, size):
    return pl.CostEstimate(flops=flops, bytes_accessed=size, transcendentals=0)


SMEM = pl.BlockSpec(memory_space=pltpu.SMEM)
VMEM = pl.BlockSpec(memory_space=pltpu.VMEM)


def onehot(hit):
    return jnp.where(hit, 1.0, 0.0).astype(BF16)


def first_row(meta, by_layer, m):
    if not by_layer:
        return lax.div(m, ROWS) * (PARTS * ROWS) + lax.rem(m, ROWS)
    total = lax.div(m, LAYERS)
    layer = lax.rem(m, LAYERS)
    for n in range(LAYERS):
        total = total + jnp.where(layer == n, meta[TO + n], 0)
    return total


def pack_kernel(by_layer, meta, *refs):
    x_refs, o_ref = refs[:-1], refs[-1]
    base = first_row(meta, by_layer, lax.broadcasted_iota(jnp.int32, (1, BLOCK), 1))
    row = lax.broadcasted_iota(jnp.int32, (PARTS * BLOCK, BLOCK), 0)
    total = None
    for q in range(PARTS):
        x = x_refs[q][...] if len(x_refs) > 1 else x_refs[0][:, q * COLS : (q + 1) * COLS]
        part = meta[PART + q] if len(x_refs) > 1 else q
        term = jnp.dot(onehot(row == base + ROWS * part), x, preferred_element_type=F32)
        total = term if total is None else total + term
    o_ref[...] = total.astype(BF16)


def pack(meta, by_layer, xs):
    return pl.pallas_call(
        functools.partial(pack_kernel, by_layer),
        out_shape=jax.ShapeDtypeStruct((PARTS * BLOCK, COLS), BF16),
        in_specs=[SMEM] + [VMEM] * len(xs),
        out_specs=VMEM,
        compiler_params=params(8),
        cost_estimate=cost(2 * BLOCK * BLOCK * WIDE * 4, 4 * BLOCK * WIDE),
        name="pack",
    )(meta, *xs)


def unpack_kernel(by_layer, interleave, meta, x_ref, o_ref):
    base = first_row(meta, by_layer, lax.broadcasted_iota(jnp.int32, (BLOCK, 1), 0))
    col = lax.broadcasted_iota(jnp.int32, (BLOCK, PARTS * BLOCK), 1)
    for q in range(PARTS):
        block = jnp.dot(onehot(col == base + ROWS * q), x_ref[...], preferred_element_type=F32).astype(BF16)
        if not interleave:
            o_ref[:, q * COLS : (q + 1) * COLS] = block
            continue
        xh, c = q // 2, q % 2
        for y in range(4):
            at = (xh * 8 + y * 2 + c) * BLOCK
            o_ref[:, at : at + BLOCK] = block[:, y * BLOCK : (y + 1) * BLOCK]


def unpack(meta, by_layer, interleave, x):
    return pl.pallas_call(
        functools.partial(unpack_kernel, by_layer, interleave),
        out_shape=jax.ShapeDtypeStruct((BLOCK, WIDE), BF16),
        in_specs=[SMEM, VMEM],
        out_specs=VMEM,
        compiler_params=params(8),
        cost_estimate=cost(2 * BLOCK * BLOCK * WIDE * 4, 4 * BLOCK * WIDE),
        name="unpack",
    )(meta, x)


def place_kernel(meta, *refs):
    x_refs, (o_ref, sem) = refs[:-2], refs[-2:]
    copies = [
        pltpu.make_async_copy(x, o_ref.at[pl.ds(pl.multiple_of(meta[BAT + n], 16), x.shape[0])], sem.at[n])
        for n, x in enumerate(x_refs)
    ]
    for copy in copies:
        copy.start()
    for copy in copies:
        copy.wait()


def place(meta, xs):
    rows = sum(x.shape[0] for x in xs)
    return pl.pallas_call(
        place_kernel,
        out_shape=jax.ShapeDtypeStruct((rows, WIDE), BF16),
        in_specs=[SMEM] + [pl.BlockSpec(memory_space=pltpu.HBM)] * len(xs),
        out_specs=VMEM,
        scratch_shapes=[pltpu.SemaphoreType.DMA((len(xs),))],
        compiler_params=params(4),
        cost_estimate=cost(10000000000, 4 * rows * WIDE),
        name="place",
    )(meta, *xs)


def right_kernel(count, b_ref, *refs):
    g_refs, (o, g_all) = refs[:count], refs[count:]
    for n, g in enumerate(g_refs):
        g_all[n * BLOCK : (n + 1) * BLOCK] = g[...]
    o[...] = lax.dot_general(
        g_all[...], b_ref[...], (((1,), (1,)), ((), ())), preferred_element_type=F32
    ).astype(BF16)


def right(gs, b):
    n = len(gs)
    return pl.pallas_call(
        functools.partial(right_kernel, n),
        out_shape=jax.ShapeDtypeStruct((n * BLOCK, COLS), BF16),
        in_specs=[VMEM] + [VMEM] * n,
        out_specs=VMEM,
        scratch_shapes=[pltpu.VMEM((n * BLOCK, WIDE), BF16)],
        compiler_params=params(8),
        cost_estimate=cost(2 * n * BLOCK * COLS * WIDE, 2 * (n * BLOCK + COLS) * WIDE),
        name="right",
    )(b, *gs)


def left_kernel(side, meta, *refs):
    a_refs, r_refs = refs[:4], refs[4:8]
    a_all, r_all = refs[-2:]
    columns = pl.ds(pl.multiple_of(meta[SIDE + side], 128), WIDE // 2)
    for n, a in enumerate(a_refs):
        a_all[n * BLOCK : (n + 1) * BLOCK] = a[:, columns]
    for n, r in enumerate(r_refs):
        for k in range(2):
            to = pl.ds(pl.multiple_of(meta[RAT + 8 * side + 2 * n + k], 16), BLOCK)
            r_all[to] = r[k * BLOCK : (k + 1) * BLOCK]
    total = jnp.dot(a_all[...], r_all[...], preferred_element_type=F32)
    if side == 0:
        refs[8][...] = total
        return
    total = (total + refs[8][...]).astype(BF16)
    for n, o in enumerate(refs[9:13]):
        o[...] = total[n * BLOCK : (n + 1) * BLOCK]


def left(meta, side, blocks, rs, partial=None):
    first = side == 0
    return pl.pallas_call(
        functools.partial(left_kernel, side),
        out_shape=jax.ShapeDtypeStruct((COLS, COLS), F32)
        if first
        else [jax.ShapeDtypeStruct((BLOCK, COLS), BF16)] * 4,
        in_specs=[SMEM] + [VMEM] * 8 + ([] if first else [VMEM]),
        out_specs=VMEM if first else [VMEM] * 4,
        scratch_shapes=[
            pltpu.VMEM((COLS, WIDE // 2), BF16),
            pltpu.VMEM((WIDE // 2, COLS), BF16),
        ],
        compiler_params=params(10),
        cost_estimate=cost(COLS * COLS * WIDE, 4 * COLS * WIDE),
        name="left",
    )(meta, *blocks, *rs, *([] if first else [partial]))


def along_y(value):
    return [value, shift(value, "y", 1), shift(value, "y", -1), shift(value, "y", 2)]


def exchange(x):
    x = x.reshape(LAYERS, PARTS * ROWS, COLS)
    return lax.all_to_all(x, DP, split_axis=0, concat_axis=0, tiled=True).reshape(-1, COLS)


def after(value, *others):
    return lax.optimization_barrier((value, others))[0]


def local(gradient, owner, a_inverse, b_inverse):
    xh, y, c = (lax.axis_index(n) for n in ("xh", "y", "c"))
    a, b = a_inverse[0], b_inverse[0]
    ys = [y, (y + 3) % 4, (y + 1) % 4, (y + 2) % 4]
    near = [(xh, c), (xh, 1 - c), (1 - xh, c), (1 - xh, 1 - c)]
    scalars = [u * 2 + w for u, w in near]
    scalars += [v * BLOCK for v in ys] + [ys[3] * BLOCK + BLOCK // 2]
    scalars += [(v * 2 + w) * BLOCK for v in ys for w in (c, 1 - c)] * 2
    scalars += [xh * (WIDE // 2), (1 - xh) * (WIDE // 2)]
    meta = jnp.concatenate([owner * (PARTS * ROWS), jnp.stack(scalars)]).astype(jnp.int32)

    half = BLOCK // 2
    up, down = shift(b, "y", 1), shift(b, "y", -1)
    bs = [b, up, down, shift(up[:half], "y", 1), shift(down[half:], "y", -1)]
    rows = gradient.transpose(1, 0, 2).reshape(BLOCK, WIDE)
    packed = pack(meta, True, [rows])
    a = after(a, packed)
    over = flip(a, 2)
    blocks = [a, flip(a, 1), over, flip(over, 1)]
    got, b, blocks = lax.optimization_barrier((exchange(packed), place(meta, bs), blocks))
    g = unpack(meta, False, False, got)
    over = flip(g, 2)
    r = right([g, flip(g, 1)], b)
    first = along_y(r)
    over = after(over, first)
    second = along_y(right([over, flip(over, 1)], b))
    partial = left(meta, 0, blocks, first)
    out = left(meta, 1, blocks, second, partial)
    mine = [out[0]] + [flip(out[mask], mask) for mask in range(1, 4)]
    done = unpack(meta, True, True, exchange(pack(meta, False, mine)))
    return done.reshape(ROWS, LAYERS, WIDE).transpose(1, 0, 2)


def solution(mesh):
    fine = Mesh(mesh.devices.reshape(tuple(SIZES[n] for n in AXES)), AXES)
    rows = ("xh", "y", "c")
    in_specs = (P(None, rows + DP, None), P(), P(DP, rows, None), P(DP, rows, None))
    return jax.shard_map(
        local, mesh=fine, in_specs=in_specs, out_specs=P(None, rows + DP, None), check_vma=False
    )
```
